256 devices in a mesh: domain: 32 (over z, y_hi, core), band: 8 (over x, y_lo).
Axes of the slice: x: 4, y: 4 (y_hi: 2, y_lo: 2; y = y_hi * 2 + y_lo), z: 8, core: 2. Of those that a mesh axis runs over, the one named last changes fastest.
Arguments:
- orbitals: float32 [32, 192, 36864], P('band', 'domain'), may hold values from -6 to 6
- potential: float32 [192, 36864], P('domain'), may hold values from -1.5 to 1.5
- coefficients: float32 [32, 32], replicated, may hold values from -1.75 to 1.75
- owners: int32 [2], replicated, may hold values from 0 to 31
Outputs:
- filtered: float32 [32, 192, 36864], P('band', 'domain')
- rotated: float32 [32, 192, 36864], P('band', 'domain')
The draws below stay inside these ranges and needn't reach their ends.
All inputs are finite; a program needn't handle non-finite values.
Results may differ from the reference program's by a relative error of at most 0.0001.
Values sent between devices are 32-bit elements; how exact they have to be, the bound alone decides.
No kernel may reach another device: no remote copies, remote signals or barrier semaphores. Data moves between devices by JAX's collectives and lax.ppermute only.
A program may use at most 256 MiB of HBM per device.

```python
import jax
import jax.numpy as jnp
from jax import lax

B_DEV = 4
NZ = 192
PLANE = 36864
DEG = 3
ROUNDS = 2
NX = 192
NB = 32
N_BAND = 8


def shard_levels(rng, extent, shards, smallest, top_value):
    level, own = 1.0, jax.random.fold_in(rng, 6)
    for axis_at, blocks in shards:
        draws = jnp.exp(jax.random.uniform(jax.random.fold_in(own, axis_at), (blocks,), jnp.float32, smallest / len(shards), top_value / len(shards)))
        level = level * jnp.repeat(draws, extent[axis_at] // blocks).reshape([-1 if axis == axis_at else 1 for axis in range(len(extent))])
    return level


def bell_draw(own_key, dims, spread, reach, cuts=(), kind=jnp.bfloat16):
    loudness = shard_levels(own_key, dims, cuts, -0.22, 0.18) if cuts else 1.0
    drawn = jax.random.normal(own_key, dims, jnp.float32) * spread * loudness
    return jnp.minimum(jnp.maximum(drawn, -reach), reach).astype(kind)


def setup_inputs(seed: int = 0) -> dict:
    key_of = jax.random.split(jax.random.key(seed), 5)
    return {
        "orbitals": bell_draw(key_of[0], (NB, NX, PLANE), 1.0, 6.0, ((0, 8), (1, 32)), jnp.float32),
        "potential": jnp.clip(jax.random.uniform(key_of[1], (NX, PLANE), jnp.float32, -1.5, 1.5) * shard_levels(key_of[1], (NX, PLANE), ((0, 32),), -0.4, 0.0), -1.5, 1.5),
        "coefficients": bell_draw(key_of[2], (NB, NB), (B_DEV * (1 + ROUNDS)) ** -0.5, 1.75, (), jnp.float32),
        "owners": jax.random.randint(key_of[3], (ROUNDS,), 0, NB).astype(jnp.int32),
    }


lap_coeffs = (-205.0 / 72.0, 8.0 / 5.0, -1.0 / 5.0, 8.0 / 315.0, -1.0 / 560.0)


def hamiltonian(field, potential):
    cells_x = field.shape[1]
    plane = field.shape[2]
    column_z = jnp.arange(plane).astype(jnp.int32) % NZ
    padded_x = jnp.pad(field, ((0, 0), (4, 4), (0, 0)), mode="wrap")
    padded_y = jnp.pad(field, ((0, 0), (0, 0), (4 * NZ, 4 * NZ)))
    padded_z = jnp.pad(field, ((0, 0), (0, 0), (4, 4)))
    summed = 3.0 * lap_coeffs[0] * field
    for shift in range(1, 5):
        weight_k = lap_coeffs[shift]
        upper_ok = (column_z + shift < NZ).astype(field.dtype)
        lower_ok = (column_z - shift >= 0).astype(field.dtype)
        summed = summed + weight_k * (padded_x[:, 4 + shift:4 + shift + cells_x] + padded_x[:, 4 - shift:4 - shift + cells_x])
        summed = summed + weight_k * (padded_y[:, :, (4 + shift) * NZ:(4 + shift) * NZ + plane] + padded_y[:, :, (4 - shift) * NZ:(4 - shift) * NZ + plane])
        summed = summed + weight_k * (padded_z[:, :, 4 + shift:4 + shift + plane] * upper_ok + padded_z[:, :, 4 - shift:4 - shift + plane] * lower_ok)
    return -0.5 * summed + potential[None] * field


def chebyshev(block, potential):
    previous = block
    current = (hamiltonian(block, potential) - 6.0 * block) / 5.0
    for level in range(DEG - 1):
        following = 2.0 * (hamiltonian(current, potential) - 6.0 * current) / 5.0 - previous
        previous = current
        current = following
    return current


def reference(orbitals, potential, coefficients, owners):
    blocks = orbitals.reshape(N_BAND, B_DEV, NX, PLANE)

    def filter_block(single_block):
        return chebyshev(single_block, potential)

    filtered = lax.map(filter_block, blocks)
    coeff_blocks = coefficients.reshape(N_BAND, B_DEV, N_BAND, B_DEV)

    def rotate_block(index):
        summed = jnp.einsum("bxp,bc->cxp", filtered[index], coeff_blocks[index, :, index, :], precision=lax.Precision.HIGHEST)
        for turn in range(ROUNDS):
            source = owners[turn] // B_DEV
            offset = owners[turn] % B_DEV
            rolled = jnp.roll(filtered[source], -offset, axis=0)
            summed = summed + jnp.einsum("bxp,bc->cxp", rolled, coeff_blocks[source, :, index, :], precision=lax.Precision.HIGHEST)
        return summed

    rotated = lax.map(rotate_block, jnp.arange(N_BAND).astype(jnp.int32))
    return filtered.reshape(NB, NX, PLANE), rotated.reshape(NB, NX, PLANE)
```

```python
import jax
import jax.numpy as jnp
from jax import lax
from jax.sharding import PartitionSpec as P

NZ = 192
DEG = 3


lap_coeffs = (-205.0 / 72.0, 8.0 / 5.0, -1.0 / 5.0, 8.0 / 315.0, -1.0 / 560.0)


def extended_2(x, sides, width):
    for axis, dim in sides:
        peers, length = (lax.axis_size(axis), x.shape[dim])
        up = [(i, (i + 1) % peers) for i in range(peers)]
        down = [(j, i) for i, j in up]
        last = lax.slice_in_dim(x, length - width, length, axis=dim)
        first = lax.slice_in_dim(x, 0, width, axis=dim)
        before = lax.ppermute(last, axis, up)
        after = lax.ppermute(first, axis, down)
        x = jnp.concatenate([before, x, after], axis=dim)
    return x


def hamiltonian(field, extended, potential):
    cells_x = field.shape[1]
    plane = field.shape[2]
    column_z = jnp.arange(plane) % NZ
    padded_y = jnp.pad(field, ((0, 0), (0, 0), (4 * NZ, 4 * NZ)))
    padded_z = jnp.pad(field, ((0, 0), (0, 0), (4, 4)))
    summed = 3.0 * lap_coeffs[0] * field
    for shift in range(1, 5):
        weight_k = lap_coeffs[shift]
        upper_ok = (column_z + shift < NZ).astype(field.dtype)
        lower_ok = (column_z - shift >= 0).astype(field.dtype)
        summed = summed + weight_k * (
            extended[:, 4 + shift : 4 + shift + cells_x]
            + extended[:, 4 - shift : 4 - shift + cells_x]
        )
        summed = summed + weight_k * (
            padded_y[:, :, (4 + shift) * NZ : (4 + shift) * NZ + plane]
            + padded_y[:, :, (4 - shift) * NZ : (4 - shift) * NZ + plane]
        )
        summed = summed + weight_k * (
            padded_z[:, :, 4 + shift : 4 + shift + plane] * upper_ok
            + padded_z[:, :, 4 - shift : 4 - shift + plane] * lower_ok
        )
    return -0.5 * summed + potential[None] * field


def chebyshev(block, potential, widen):
    previous = block
    current = (hamiltonian(block, widen(block), potential) - 6.0 * block) / 5.0
    for level in range(DEG - 1):
        following = (
            2.0 * (hamiltonian(current, widen(current), potential) - 6.0 * current) / 5.0 - previous
        )
        previous = current
        current = following
    return current


def widen_own(field):
    return extended_2(field, (("domain", 1),), 4)


def mixing_matrix(coefficients, owners, width):
    rows = jnp.arange(coefficients.shape[0])
    same = (rows[:, None] // width) == (rows[None, :] // width)
    mixed = jnp.where(same, coefficients, 0.0)
    for turn in range(owners.shape[0]):
        source = owners[turn] // width
        offset = owners[turn] % width
        member = (rows // width == source)[:, None]
        from_row = source * width + (rows % width - offset) % width
        picks = (from_row[:, None] == rows[None, :]).astype(coefficients.dtype)
        part = jnp.dot(picks, coefficients, precision=lax.Precision.HIGHEST)
        mixed = mixed + jnp.where(member, part, 0.0)
    return mixed


def body(orbitals, potential, coefficients, owners):
    width, planes, cells = orbitals.shape
    bands = lax.axis_size("band")
    filtered = chebyshev(orbitals, potential, widen_own)
    mixed = mixing_matrix(coefficients, owners, width).reshape(bands, width, bands, width)
    parts = filtered.reshape(width, planes, bands, cells // bands)
    gathered = lax.all_to_all(parts, "band", 2, 0)
    turned = jnp.einsum("iqxp,iqjo->joxp", gathered, mixed, precision=lax.Precision.HIGHEST)
    rotated = lax.all_to_all(turned, "band", 0, 2)
    return (filtered, rotated.reshape(width, planes, cells))


def solution(mesh):
    in_specs = (P("band", "domain", None), P("domain", None), P(), P())
    out_specs = (P("band", "domain", None), P("band", "domain", None))
    return jax.shard_map(body, mesh=mesh, in_specs=in_specs, out_specs=out_specs, check_vma=False)
```

```python
import functools

import jax
import jax.numpy as jnp
import numpy as np
from jax import lax
from jax.experimental import pallas as pl
from jax.experimental.pallas import tpu as pltpu
from jax.sharding import PartitionSpec as P


NZ = 192
lap_coeffs = (-205.0 / 72.0, 8.0 / 5.0, -1.0 / 5.0, 8.0 / 315.0, -1.0 / 560.0)
weights = tuple(-0.1 * value for value in lap_coeffs)


def along_z():
    cell = lax.broadcasted_iota(jnp.int32, (384, 384), 0)
    other = lax.broadcasted_iota(jnp.int32, (384, 384), 1)
    apart = jnp.abs(cell - other)
    same = (cell < NZ) == (other < NZ)
    parts = [jnp.zeros((384, 384), jnp.bfloat16)] * 2
    for k in range(1, 5):
        rounded = np.float32(weights[k]).astype(jnp.bfloat16)
        rest = np.float32(weights[k] - float(rounded)).astype(jnp.bfloat16)
        parts = [jnp.where((apart == k) & same, value, part) for value, part in zip((rounded, rest), parts)]
    return jnp.concatenate([parts[0], parts[0], parts[1]], axis=0)


def inner_kernel(own, scaled, line, *rest, group, first):
    if first:
        out, field, half, even, odd = rest
        before = None
    else:
        before, out, field, half, even, odd = rest
    planes, rows, _ = own.shape
    pad = 24 * group
    step = 3 * group
    blocks = rows // pad
    zeros = jnp.zeros((pad, 128), jnp.float32)
    left = lax.broadcasted_iota(jnp.int32, (8, 128), 1) < 64

    def strided(ref, x, at):
        return ref[x, pl.ds(at, 8, stride=step), :]

    for x in range(planes):
        field[x, 0:pad] = zeros
        field[x, pad + rows :] = zeros
        half[x, pad + rows :] = zeros

    def fill(i, carry):
        at = pl.multiple_of(i * pad, 8)
        for x in range(planes):
            field[x, pl.ds(pad + at, pad), :] = own[x, pl.ds(at, pad), :]
        return carry

    lax.fori_loop(0, blocks, fill, 0)

    def halve(i, carry):
        for x in range(planes):
            for o in range(group):
                tiles = [strided(field, x, i * pad + a * group + o) for a in range(4)]
                for a in range(3):
                    turned = pltpu.roll(jnp.where(left, tiles[a + 1], tiles[a]), 64, 1)
                    half[x, pl.ds(i * pad + a * group + o, 8, stride=step), :] = turned
        return carry

    lax.fori_loop(0, blocks + 1, halve, 0)

    def multiply(i):
        pieces = [
            jnp.concatenate(
                [strided(own, x, i * pad + a * group + o) for x in range(planes) for o in range(group)],
                axis=0,
            )
            for a in range(3)
        ]
        exact = jnp.concatenate(pieces, axis=1)
        high_part = exact.astype(jnp.bfloat16)
        low_part = (exact - high_part.astype(jnp.float32)).astype(jnp.bfloat16)
        return jnp.dot(
            jnp.concatenate([high_part, low_part, high_part], axis=1),
            line[...],
            preferred_element_type=jnp.float32,
        )

    def compute(i, part):
        for o in range(group):
            for a in range(3):
                at = i * pad + a * group + o
                column = [strided(own, x, at) for x in range(planes)]
                for x in range(planes):

                    def near(ref, tiles):
                        return strided(ref, x, pad + at + tiles * group)

                    row = (x * group + o) * 8
                    total = part[row : row + 8, 128 * a : 128 * a + 128]
                    total = total + scaled[x, pl.ds(i * 24 + a, 8, stride=3), :] * column[x]
                    pairs = (
                        near(half, 1) + near(half, -2),
                        near(field, 3) + near(field, -3),
                        near(half, 4) + near(half, -5),
                        near(field, 6) + near(field, -6),
                    )
                    for k in range(1, 5):
                        around = pairs[k - 1]
                        if x - k >= 0:
                            around = around + column[x - k]
                        if x + k < planes:
                            around = around + column[x + k]
                        total = total + weights[k] * around
                    if not first:
                        total = 2.0 * total - strided(before, x, at)
                    out[x, pl.ds(at, 8, stride=step), :] = total

    even[...] = multiply(0)

    def pair(i, carry):
        odd[...] = multiply(2 * i + 1)
        compute(2 * i, even)
        even[...] = multiply(jnp.minimum(2 * i + 2, blocks - 1))
        compute(2 * i + 1, odd)
        return carry

    lax.fori_loop(0, blocks // 2, pair, 0)


def inner(own, scaled, line, before, group):
    planes, rows, _ = own.shape
    first = before is None
    operands = (own, scaled, line) + (() if first else (before,))
    padded = (planes, rows + 48 * group, 128)
    return pl.pallas_call(
        functools.partial(inner_kernel, group=group, first=first),
        out_shape=jax.ShapeDtypeStruct(own.shape, jnp.float32),
        in_specs=[pl.BlockSpec(memory_space=pltpu.VMEM)] * len(operands),
        out_specs=pl.BlockSpec(memory_space=pltpu.VMEM),
        scratch_shapes=[
            pltpu.VMEM(padded, jnp.float32),
            pltpu.VMEM(padded, jnp.float32),
            pltpu.VMEM((planes * group * 8, 384), jnp.float32),
            pltpu.VMEM((planes * group * 8, 384), jnp.float32),
        ],
        name="inner_first" if first else "inner_next",
    )(*operands)


def edge_kernel(partial, low, top, out, *, factor):
    rows = partial.shape[1]

    def add(halo, nearby):
        def body(i, carry):
            at = pl.ds(pl.multiple_of(i * 8, 8), 8)
            beyond = [halo[x, at, :] for x in range(4)]
            for x in range(4):
                total = partial[x, at, :]
                for k in range(1, 5):
                    if nearby(x, k) is not None:
                        total = total + (factor * weights[k]) * beyond[nearby(x, k)]
                out[x, at, :] = total
            return carry

        lax.fori_loop(0, rows // 8, body, 0, unroll=4)

    @pl.when(pl.program_id(0) == 0)
    def _():
        add(low, lambda x, k: 4 + x - k if x < k else None)

    @pl.when(pl.program_id(0) == 1)
    def _():
        add(top, lambda x, k: x + k - 4 if x + k > 3 else None)


def edges(partial, low, top, factor):
    planes, rows, _ = partial.shape
    end = pl.BlockSpec((4, rows, 128), lambda i: (i * (planes // 4 - 1), 0, 0))
    halo = pl.BlockSpec((4, rows, 128), lambda i: (0, 0, 0))
    return pl.pallas_call(
        functools.partial(edge_kernel, factor=factor),
        grid=(2,),
        out_shape=jax.ShapeDtypeStruct(partial.shape, jnp.float32),
        in_specs=[end, halo, halo],
        out_specs=end,
        input_output_aliases={0: 0},
        name="edges",
    )(partial, low, top)


def rotate_kernel(source, mixing, field, out):
    bands, rows, _ = field.shape
    step = 8

    def body(i, carry):
        base = i * (step * 4)

        def orbital(band, q):
            return field[band, pl.ds(base + q, step, stride=4), :]

        shared = [orbital(source[t], q) for t in range(2) for q in range(4)]
        for band in range(bands):
            own = [orbital(band, q) for q in range(4)]
            for o in range(4):
                total = mixing[0, band, 0, o] * own[0]
                for q in range(1, 4):
                    total = total + mixing[0, band, q, o] * own[q]
                for t in range(2):
                    for q in range(4):
                        total = total + mixing[1 + t, band, q, o] * shared[4 * t + q]
                out[band, pl.ds(base + o, step, stride=4), :] = total
        return carry

    lax.fori_loop(0, rows // (step * 4), body, 0)


def rotate(source, mixing, field):
    return pl.pallas_call(
        rotate_kernel,
        out_shape=jax.ShapeDtypeStruct(field.shape, jnp.float32),
        in_specs=[
            pl.BlockSpec(memory_space=pltpu.SMEM),
            pl.BlockSpec(memory_space=pltpu.SMEM),
            pl.BlockSpec(memory_space=pltpu.VMEM),
        ],
        out_specs=pl.BlockSpec(memory_space=pltpu.VMEM),
        name="rotate",
    )(source, mixing, field)


AXES = ("domain", "band")


def split_kernel(orbit, rows, *outs):
    tiles = outs[0].shape[1]

    def body(i, carry):
        at = pl.ds(pl.multiple_of(i * 8, 8), 8)
        for k, out in enumerate(outs):
            out[0, at, :] = rows[0, pl.ds(i * 32 + orbit[k], 8, stride=4), :]
        return carry

    lax.fori_loop(0, tiles // 8, body, 0, unroll=4)


def split(orbit, rows):
    planes, count, _ = rows.shape
    small = pl.BlockSpec((1, count // 4, 128), lambda x: (x, 0, 0))
    return pl.pallas_call(
        split_kernel,
        grid=(planes,),
        out_shape=[jax.ShapeDtypeStruct((planes, count // 4, 128), jnp.float32)] * 4,
        in_specs=[pl.BlockSpec(memory_space=pltpu.SMEM), pl.BlockSpec((1, count, 128), lambda x: (x, 0, 0))],
        out_specs=[small] * 4,
        name="split",
    )(orbit, rows)


def merge_kernel(orbit, *refs):
    out = refs[-1]
    tiles = refs[0].shape[1]

    def body(i, carry):
        at = pl.ds(pl.multiple_of(i * 8, 8), 8)
        for k, part in enumerate(refs[:-1]):
            out[0, pl.ds(i * 32 + orbit[k], 8, stride=4), :] = part[0, at, :]
        return carry

    lax.fori_loop(0, tiles // 8, body, 0, unroll=4)


def merge(orbit, parts):
    planes, tiles, _ = parts[0].shape
    small = pl.BlockSpec((1, tiles, 128), lambda x: (x, 0, 0))
    return pl.pallas_call(
        merge_kernel,
        grid=(planes,),
        out_shape=jax.ShapeDtypeStruct((planes, tiles * 4, 128), jnp.float32),
        in_specs=[pl.BlockSpec(memory_space=pltpu.SMEM)] + [small] * 4,
        out_specs=pl.BlockSpec((1, tiles * 4, 128), lambda x: (x, 0, 0)),
        name="merge",
    )(orbit, *parts)


def place_kernel(slot, *refs):
    out, sems = refs[-2], refs[-1]
    planes = refs[0].shape[0]
    copies = [
        pltpu.make_async_copy(part, out.at[pl.ds(slot[k] * planes, planes)], sems.at[k])
        for k, part in enumerate(refs[:-2])
    ]
    for copy in copies:
        copy.start()
    for copy in copies:
        copy.wait()


def place(slot, parts):
    planes, tiles, _ = parts[0].shape
    return pl.pallas_call(
        place_kernel,
        out_shape=jax.ShapeDtypeStruct((planes * 4, tiles, 128), jnp.float32),
        in_specs=[pl.BlockSpec(memory_space=pltpu.SMEM)] + [pl.BlockSpec(memory_space=pl.ANY)] * 4,
        out_specs=pl.BlockSpec(memory_space=pltpu.VMEM),
        scratch_shapes=[pltpu.SemaphoreType.DMA((4,))],
        name="place",
    )(slot, *parts)


def route(move):
    def at(x, y, z, c):
        return (z * 4 + y // 2 * 2 + c) * 8 + x * 2 + y % 2

    pairs = []
    for z in range(8):
        for y in range(4):
            for c in range(2):
                for x in range(4):
                    to_x, to_y, to_z, to_c = move(x, y, z, c)
                    pairs.append((at(x, y, z, c), at(to_x % 4, to_y % 4, to_z % 8, to_c % 2)))
    return pairs


def send(value, move):
    return lax.ppermute(value, AXES, route(move))


STEPS = ((1, 0), (1, 1), (-1, 0), (-1, 1))
ORBIT = np.array(
    [[[(y + dy) % 4 // 2 * 2 + (c + dc) % 2 for dy, dc in STEPS] for c in range(2)] for y in range(4)],
    np.int32,
)
SLOT = np.array(
    [[[(y - dy) % 4 // 2 * 2 + (c + dc) % 2 for dy, dc in STEPS] for c in range(2)] for y in range(4)],
    np.int32,
)


def whole_potential(slab, chip_x, high, core):
    planes, tiles, _ = slab.shape
    part = planes * tiles // 4
    mine = lax.dynamic_slice_in_dim(slab.reshape(4 * part, 128), chip_x * part, part)
    there = send(mine, lambda x, y, z, c: (x, y + (1 if y % 2 else -1), z, c))
    pieces = [there] + [send(there, lambda x, y, z, c, k=k: (x + k, y, z, c)) for k in range(1, 4)]
    stacked = jnp.stack(pieces)
    other = jnp.concatenate([lax.dynamic_index_in_dim(stacked, (chip_x - k) % 4, 0, False) for k in range(4)])
    other = other.reshape(slab.shape)
    both = jnp.where(high == 0, jnp.stack([slab, other]), jnp.stack([other, slab]))
    across = send(both, lambda x, y, z, c: (x, y, z, c + 1))
    cores = jnp.where(core == 0, jnp.stack([both, across], 1), jnp.stack([across, both], 1))
    return cores.reshape(4 * planes, tiles, 128)


def to_rows(block):
    width, planes, cells = block.shape
    tiles = block.reshape(width, planes, cells // 128, 128)
    return tiles.transpose(1, 2, 0, 3).reshape(planes, cells // 128 * width, 128)


def from_rows(rows, width):
    planes, count, _ = rows.shape
    tiles = rows.reshape(planes, count // width, width, 128).transpose(2, 0, 1, 3)
    return tiles.reshape(width, planes, count // width * 128)


def mixing_weights(coefficients, owners, width, bands):
    cut = coefficients.reshape(bands, width, bands, width)
    own = jnp.stack([cut[band, :, band, :] for band in range(bands)])
    parts = [own]
    for turn in range(2):
        source, offset = owners[turn] // width, owners[turn] % width
        rows = lax.dynamic_slice(coefficients, (source * width, 0), (width, bands * width))
        rows = jnp.roll(rows, offset, axis=0)
        parts.append(rows.reshape(width, bands, width).transpose(1, 0, 2))
    return jnp.stack(parts)


def body(orbitals, potential, coefficients, owners):
    width, planes, cells = orbitals.shape
    bands = lax.axis_size("band")
    tiles = cells // 128
    place_d, place_b = lax.axis_index("domain"), lax.axis_index("band")
    core, high, chip_x = place_d % 2, place_d // 2 % 2, place_b // 2
    chip_y = high * 2 + place_b % 2
    orbit = jnp.asarray(ORBIT)[chip_y, core]
    slot = jnp.asarray(SLOT)[chip_y, core]

    parts = split(orbit, to_rows(orbitals))
    parts = [
        send(part, lambda x, y, z, c, dy=dy, dc=dc: (x, y + dy, z, c + dc))
        for part, (dy, dc) in zip(parts, STEPS)
    ]
    scaled = (potential - 6.0) * 0.2 - 0.3 * lap_coeffs[0]
    scaled = whole_potential(scaled.reshape(planes, tiles, 128), chip_x, high, core)
    line = along_z()
    previous, current = None, place(slot, parts)
    for factor in (1.0, 2.0, 2.0):
        low = send(current[-4:], lambda x, y, z, c: (x, y, z + 1, c))
        top = send(current[:4], lambda x, y, z, c: (x, y, z - 1, c))
        partial = inner(current, scaled, line, previous, 1)
        previous, current = current, edges(partial, low, top, factor)

    parts = [
        send(
            lax.dynamic_slice_in_dim(current, slot[k] * planes, planes),
            lambda x, y, z, c, dy=dy, dc=dc: (x, y - dy, z, c + dc),
        )
        for k, (dy, dc) in enumerate(STEPS)
    ]
    current = merge(orbit, parts)
    filtered = from_rows(current, width)
    gathered = lax.all_to_all(current.reshape(bands, planes, -1, 128), "band", 0, 0)
    mixing = mixing_weights(coefficients, owners, width, bands)
    turned = rotate(owners // width, mixing, gathered.reshape(bands, -1, 128))
    returned = lax.all_to_all(turned.reshape(bands, planes, -1, 128), "band", 0, 0)
    rotated = from_rows(returned.reshape(planes, tiles * width, 128), width)
    return (filtered, rotated)


def solution(mesh):
    in_specs = (P("band", "domain", None), P("domain", None), P(), P())
    out_specs = (P("band", "domain", None), P("band", "domain", None))
    return jax.shard_map(body, mesh=mesh, in_specs=in_specs, out_specs=out_specs, check_vma=False)
```

```python
import functools

import jax
import jax.numpy as jnp
import numpy as np
from jax import lax
from jax.experimental import pallas as pl
from jax.experimental.pallas import tpu as pltpu
from jax.sharding import PartitionSpec as P


NZ = 192
lap_coeffs = (-205.0 / 72.0, 8.0 / 5.0, -1.0 / 5.0, 8.0 / 315.0, -1.0 / 560.0)
weights = tuple(-0.1 * value for value in lap_coeffs)


def along_z():
    cell = lax.broadcasted_iota(jnp.int32, (384, 384), 0)
    other = lax.broadcasted_iota(jnp.int32, (384, 384), 1)
    apart = jnp.abs(cell - other)
    same = (cell < NZ) == (other < NZ)
    parts = [jnp.zeros((384, 384), jnp.bfloat16)] * 2
    for k in range(1, 5):
        rounded = np.float32(weights[k]).astype(jnp.bfloat16)
        rest = np.float32(weights[k] - float(rounded)).astype(jnp.bfloat16)
        parts = [jnp.where((apart == k) & same, value, part) for value, part in zip((rounded, rest), parts)]
    return jnp.concatenate([parts[0], parts[0], parts[1]], axis=0)


def inner_kernel(own, scaled, line, *rest, group, first):
    if first:
        out, field, half, even, odd = rest
        before = None
    else:
        before, out, field, half, even, odd = rest
    planes, rows, _ = own.shape
    pad = 24 * group
    step = 3 * group
    blocks = rows // pad
    zeros = jnp.zeros((pad, 128), jnp.float32)
    left = lax.broadcasted_iota(jnp.int32, (8, 128), 1) < 64

    def strided(ref, x, at):
        return ref[x, pl.ds(at, 8, stride=step), :]

    for x in range(planes):
        field[x, 0:pad] = zeros
        field[x, pad + rows :] = zeros
        half[x, pad + rows :] = zeros

    def fill(i, carry):
        at = pl.multiple_of(i * pad, 8)
        for x in range(planes):
            field[x, pl.ds(pad + at, pad), :] = own[x, pl.ds(at, pad), :]
        return carry

    lax.fori_loop(0, blocks, fill, 0)

    def halve(i, carry):
        for x in range(planes):
            for o in range(group):
                tiles = [strided(field, x, i * pad + a * group + o) for a in range(4)]
                for a in range(3):
                    turned = pltpu.roll(jnp.where(left, tiles[a + 1], tiles[a]), 64, 1)
                    half[x, pl.ds(i * pad + a * group + o, 8, stride=step), :] = turned
        return carry

    lax.fori_loop(0, blocks + 1, halve, 0)

    def multiply(i):
        pieces = [
            jnp.concatenate(
                [strided(own, x, i * pad + a * group + o) for x in range(planes) for o in range(group)],
                axis=0,
            )
            for a in range(3)
        ]
        exact = jnp.concatenate(pieces, axis=1)
        high_part = exact.astype(jnp.bfloat16)
        low_part = (exact - high_part.astype(jnp.float32)).astype(jnp.bfloat16)
        return jnp.dot(
            jnp.concatenate([high_part, low_part, high_part], axis=1),
            line[...],
            preferred_element_type=jnp.float32,
        )

    def compute(i, part):
        for o in range(group):
            for a in range(3):
                at = i * pad + a * group + o
                column = [strided(own, x, at) for x in range(planes)]
                for x in range(planes):

                    def near(ref, tiles):
                        return strided(ref, x, pad + at + tiles * group)

                    row = (x * group + o) * 8
                    total = part[row : row + 8, 128 * a : 128 * a + 128]
                    total = total + scaled[x, pl.ds(i * 24 + a, 8, stride=3), :] * column[x]
                    pairs = (
                        near(half, 1) + near(half, -2),
                        near(field, 3) + near(field, -3),
                        near(half, 4) + near(half, -5),
                        near(field, 6) + near(field, -6),
                    )
                    for k in range(1, 5):
                        around = pairs[k - 1]
                        if x - k >= 0:
                            around = around + column[x - k]
                        if x + k < planes:
                            around = around + column[x + k]
                        total = total + weights[k] * around
                    if not first:
                        total = 2.0 * total - strided(before, x, at)
                    out[x, pl.ds(at, 8, stride=step), :] = total

    even[...] = multiply(0)

    def pair(i, carry):
        odd[...] = multiply(2 * i + 1)
        compute(2 * i, even)
        even[...] = multiply(jnp.minimum(2 * i + 2, blocks - 1))
        compute(2 * i + 1, odd)
        return carry

    lax.fori_loop(0, blocks // 2, pair, 0)


def inner(own, scaled, line, before, group):
    planes, rows, _ = own.shape
    first = before is None
    operands = (own, scaled, line) + (() if first else (before,))
    padded = (planes, rows + 48 * group, 128)
    return pl.pallas_call(
        functools.partial(inner_kernel, group=group, first=first),
        out_shape=jax.ShapeDtypeStruct(own.shape, jnp.float32),
        in_specs=[pl.BlockSpec(memory_space=pltpu.VMEM)] * len(operands),
        out_specs=pl.BlockSpec(memory_space=pltpu.VMEM),
        scratch_shapes=[
            pltpu.VMEM(padded, jnp.float32),
            pltpu.VMEM(padded, jnp.float32),
            pltpu.VMEM((planes * group * 8, 384), jnp.float32),
            pltpu.VMEM((planes * group * 8, 384), jnp.float32),
        ],
        name="inner_first" if first else "inner_next",
    )(*operands)


def edge_kernel(partial, low, top, out, *, factor):
    rows = partial.shape[1]

    def add(halo, nearby):
        def body(i, carry):
            at = pl.ds(pl.multiple_of(i * 8, 8), 8)
            beyond = [halo[x, at, :] for x in range(4)]
            for x in range(4):
                total = partial[x, at, :]
                for k in range(1, 5):
                    if nearby(x, k) is not None:
                        total = total + (factor * weights[k]) * beyond[nearby(x, k)]
                out[x, at, :] = total
            return carry

        lax.fori_loop(0, rows // 8, body, 0, unroll=4)

    @pl.when(pl.program_id(0) == 0)
    def _():
        add(low, lambda x, k: 4 + x - k if x < k else None)

    @pl.when(pl.program_id(0) == 1)
    def _():
        add(top, lambda x, k: x + k - 4 if x + k > 3 else None)


def edges(partial, low, top, factor):
    planes, rows, _ = partial.shape
    end = pl.BlockSpec((4, rows, 128), lambda i: (i * (planes // 4 - 1), 0, 0))
    halo = pl.BlockSpec((4, rows, 128), lambda i: (0, 0, 0))
    return pl.pallas_call(
        functools.partial(edge_kernel, factor=factor),
        grid=(2,),
        out_shape=jax.ShapeDtypeStruct(partial.shape, jnp.float32),
        in_specs=[end, halo, halo],
        out_specs=end,
        input_output_aliases={0: 0},
        name="edges",
    )(partial, low, top)


def rotate_kernel(picked, mixing, field, *outs):
    bands = len(outs)
    tiles = field.shape[1]

    def body(i, carry):
        at = pl.ds(pl.multiple_of(i * 8, 8), 8)

        def members(band):
            return [field[q * bands + band + 1 - 2 * (band % 2), at, :] for q in range(4)]

        shared = members(picked[0]) + members(picked[1])
        for k, out in enumerate(outs):
            band = picked[2] ^ k
            own = members(band)
            for o in range(4):
                total = mixing[0, band, 0, o] * own[0]
                for q in range(1, 4):
                    total = total + mixing[0, band, q, o] * own[q]
                for t in range(2):
                    for q in range(4):
                        total = total + mixing[1 + t, band, q, o] * shared[4 * t + q]
                out[pl.ds(i * 32 + o, 8, stride=4), :] = total
        return carry

    lax.fori_loop(0, tiles // 8, body, 0)


def rotate(picked, mixing, field):
    count, tiles, _ = field.shape
    bands = count // 4
    return pl.pallas_call(
        rotate_kernel,
        out_shape=[jax.ShapeDtypeStruct((tiles * 4, 128), jnp.float32)] * bands,
        in_specs=[
            pl.BlockSpec(memory_space=pltpu.SMEM),
            pl.BlockSpec(memory_space=pltpu.SMEM),
            pl.BlockSpec(memory_space=pltpu.VMEM),
        ],
        out_specs=[pl.BlockSpec(memory_space=pltpu.VMEM)] * bands,
        name="rotate",
    )(picked, mixing, field)


AXES = ("domain", "band")


def split_kernel(orbit, rows, *outs):
    tiles = outs[0].shape[1]

    def body(i, carry):
        at = pl.ds(pl.multiple_of(i * 8, 8), 8)
        for k, out in enumerate(outs):
            out[0, at, :] = rows[0, pl.ds(i * 32 + orbit[k], 8, stride=4), :]
        return carry

    lax.fori_loop(0, tiles // 8, body, 0, unroll=4)


def split(orbit, rows):
    planes, count, _ = rows.shape
    small = pl.BlockSpec((1, count // 4, 128), lambda x: (x, 0, 0))
    return pl.pallas_call(
        split_kernel,
        grid=(planes,),
        out_shape=[jax.ShapeDtypeStruct((planes, count // 4, 128), jnp.float32)] * 4,
        in_specs=[pl.BlockSpec(memory_space=pltpu.SMEM), pl.BlockSpec((1, count, 128), lambda x: (x, 0, 0))],
        out_specs=[small] * 4,
        name="split",
    )(orbit, rows)


def merge_kernel(orbit, *refs):
    out = refs[-1]
    tiles = refs[0].shape[1]

    def body(i, carry):
        at = pl.ds(pl.multiple_of(i * 8, 8), 8)
        for k, part in enumerate(refs[:-1]):
            out[0, pl.ds(i * 32 + orbit[k], 8, stride=4), :] = part[0, at, :]
        return carry

    lax.fori_loop(0, tiles // 8, body, 0, unroll=4)


def merge(orbit, parts):
    planes, tiles, _ = parts[0].shape
    small = pl.BlockSpec((1, tiles, 128), lambda x: (x, 0, 0))
    return pl.pallas_call(
        merge_kernel,
        grid=(planes,),
        out_shape=jax.ShapeDtypeStruct((planes, tiles * 4, 128), jnp.float32),
        in_specs=[pl.BlockSpec(memory_space=pltpu.SMEM)] + [small] * 4,
        out_specs=pl.BlockSpec((1, tiles * 4, 128), lambda x: (x, 0, 0)),
        name="merge",
    )(orbit, *parts)


def place_kernel(slot, *refs):
    out, sems = refs[-2], refs[-1]
    planes = refs[0].shape[0]
    copies = [
        pltpu.make_async_copy(part, out.at[pl.ds(slot[k] * planes, planes)], sems.at[k])
        for k, part in enumerate(refs[:-2])
    ]
    for copy in copies:
        copy.start()
    for copy in copies:
        copy.wait()


def place(slot, parts):
    count, first = len(parts), parts[0].shape
    return pl.pallas_call(
        place_kernel,
        out_shape=jax.ShapeDtypeStruct((first[0] * count, *first[1:]), jnp.float32),
        in_specs=[pl.BlockSpec(memory_space=pltpu.SMEM)] + [pl.BlockSpec(memory_space=pl.ANY)] * count,
        out_specs=pl.BlockSpec(memory_space=pltpu.VMEM),
        scratch_shapes=[pltpu.SemaphoreType.DMA((count,))],
        name="place",
    )(slot, *parts)


def route(move):
    def at(x, y, z, c):
        return (z * 4 + y // 2 * 2 + c) * 8 + x * 2 + y % 2

    pairs = []
    for z in range(8):
        for y in range(4):
            for c in range(2):
                for x in range(4):
                    to_x, to_y, to_z, to_c = move(x, y, z, c)
                    pairs.append((at(x, y, z, c), at(to_x % 4, to_y % 4, to_z % 8, to_c % 2)))
    return pairs


def send(value, move):
    return lax.ppermute(value, AXES, route(move))


STEPS = ((1, 0), (1, 1), (-1, 0), (-1, 1))
ORBIT = np.array(
    [[[(y + dy) % 4 // 2 * 2 + (c + dc) % 2 for dy, dc in STEPS] for c in range(2)] for y in range(4)],
    np.int32,
)
SLOT = np.array(
    [[[(y - dy) % 4 // 2 * 2 + (c + dc) % 2 for dy, dc in STEPS] for c in range(2)] for y in range(4)],
    np.int32,
)


def whole_potential(slab, chip_x, high, core):
    planes, tiles, _ = slab.shape
    part = planes * tiles // 4
    mine = lax.dynamic_slice_in_dim(slab.reshape(4 * part, 128), chip_x * part, part)
    there = send(mine, lambda x, y, z, c: (x, y + (1 if y % 2 else -1), z, c))
    pieces = [there] + [send(there, lambda x, y, z, c, k=k: (x + k, y, z, c)) for k in range(1, 4)]
    stacked = jnp.stack(pieces)
    other = jnp.concatenate([lax.dynamic_index_in_dim(stacked, (chip_x - k) % 4, 0, False) for k in range(4)])
    other = other.reshape(slab.shape)
    both = jnp.where(high == 0, jnp.stack([slab, other]), jnp.stack([other, slab]))
    across = send(both, lambda x, y, z, c: (x, y, z, c + 1))
    cores = jnp.where(core == 0, jnp.stack([both, across], 1), jnp.stack([across, both], 1))
    return cores.reshape(4 * planes, tiles, 128)


def to_rows(block):
    width, planes, cells = block.shape
    tiles = block.reshape(width, planes, cells // 128, 128)
    return tiles.transpose(1, 2, 0, 3).reshape(planes, cells // 128 * width, 128)


def from_rows(rows, width):
    planes, count, _ = rows.shape
    tiles = rows.reshape(planes, count // width, width, 128).transpose(2, 0, 1, 3)
    return tiles.reshape(width, planes, count // width * 128)


def mixing_weights(coefficients, owners, width, bands):
    cut = coefficients.reshape(bands, width, bands, width)
    own = jnp.stack([cut[band, :, band, :] for band in range(bands)])
    parts = [own]
    for turn in range(2):
        source, offset = owners[turn] // width, owners[turn] % width
        rows = lax.dynamic_slice(coefficients, (source * width, 0), (width, bands * width))
        rows = jnp.roll(rows, offset, axis=0)
        parts.append(rows.reshape(width, bands, width).transpose(1, 0, 2))
    return jnp.stack(parts)


def body(orbitals, potential, coefficients, owners):
    width, planes, cells = orbitals.shape
    bands = lax.axis_size("band")
    tiles = cells // 128
    place_d, place_b = lax.axis_index("domain"), lax.axis_index("band")
    core, high, chip_x = place_d % 2, place_d // 2 % 2, place_b // 2
    chip_y = high * 2 + place_b % 2
    orbit = jnp.asarray(ORBIT)[chip_y, core]
    slot = jnp.asarray(SLOT)[chip_y, core]

    parts = split(orbit, to_rows(orbitals))
    parts = [
        send(part, lambda x, y, z, c, dy=dy, dc=dc: (x, y + dy, z, c + dc))
        for part, (dy, dc) in zip(parts, STEPS)
    ]
    scaled = (potential - 6.0) * 0.2 - 0.3 * lap_coeffs[0]
    scaled = whole_potential(scaled.reshape(planes, tiles, 128), chip_x, high, core)
    line = along_z()
    previous, current = None, place(slot, parts)
    for factor in (1.0, 2.0, 2.0):
        low = send(current[-4:], lambda x, y, z, c: (x, y, z + 1, c))
        top = send(current[:4], lambda x, y, z, c: (x, y, z - 1, c))
        partial = inner(current, scaled, line, previous, 1)
        previous, current = current, edges(partial, low, top, factor)

    layer = [[first + k for k in range(4 * bands)] for first in range(0, 32 * bands, 4 * bands)]
    gathered = lax.all_to_all(
        current.reshape(4 * bands, -1, 128), AXES, 0, 0, axis_index_groups=layer, tiled=True
    )
    mixing = mixing_weights(coefficients, owners, width, bands)
    picked = jnp.concatenate([owners // width, place_b[None].astype(jnp.int32)])
    turned = rotate(picked, mixing, gathered)
    parts = [
        send(
            lax.dynamic_slice_in_dim(current, slot[k] * planes, planes),
            lambda x, y, z, c, dy=dy, dc=dc: (x, y - dy, z, c + dc),
        )
        for k, (dy, dc) in enumerate(STEPS)
    ]
    homes = list(turned)
    for k in (1, 3, 5, 7, 2, 4, 6):
        homes[k] = lax.ppermute(turned[k], "band", [(i, i ^ k) for i in range(bands)])
    filtered = from_rows(merge(orbit, parts), width)
    rotated = place(jnp.arange(bands, dtype=jnp.int32) ^ place_b.astype(jnp.int32), homes)
    rotated = from_rows(rotated.reshape(planes, tiles * width, 128), width)
    return (filtered, rotated)


def solution(mesh):
    in_specs = (P("band", "domain", None), P("domain", None), P(), P())
    out_specs = (P("band", "domain", None), P("band", "domain", None))
    return jax.shard_map(body, mesh=mesh, in_specs=in_specs, out_specs=out_specs, check_vma=False)
```

```python
import functools

import jax
import jax.numpy as jnp
import numpy as np
from jax import lax
from jax.experimental import pallas as pl
from jax.experimental.pallas import tpu as pltpu
from jax.sharding import PartitionSpec as P


NZ = 192
lap_coeffs = (-205.0 / 72.0, 8.0 / 5.0, -1.0 / 5.0, 8.0 / 315.0, -1.0 / 560.0)
weights = tuple(-0.1 * value for value in lap_coeffs)


def along_z():
    cell = lax.broadcasted_iota(jnp.int32, (384, 384), 0)
    other = lax.broadcasted_iota(jnp.int32, (384, 384), 1)
    apart = jnp.abs(cell - other)
    same = (cell < NZ) == (other < NZ)
    parts = [jnp.zeros((384, 384), jnp.bfloat16)] * 2
    for k in range(1, 5):
        rounded = np.float32(weights[k]).astype(jnp.bfloat16)
        rest = np.float32(weights[k] - float(rounded)).astype(jnp.bfloat16)
        parts = [jnp.where((apart == k) & same, value, part) for value, part in zip((rounded, rest), parts)]
    return jnp.concatenate([parts[0], parts[0], parts[1]], axis=0)


def inner_kernel(own, scaled, line, *rest, group, first):
    if first:
        out, field, half, even, odd = rest
        before = None
    else:
        before, out, field, half, even, odd = rest
    planes, rows, _ = own.shape
    pad = 24 * group
    step = 3 * group
    blocks = rows // pad
    zeros = jnp.zeros((pad, 128), jnp.float32)
    left = lax.broadcasted_iota(jnp.int32, (8, 128), 1) < 64

    def strided(ref, x, at):
        return ref[x, pl.ds(at, 8, stride=step), :]

    for x in range(planes):
        field[x, 0:pad] = zeros
        field[x, pad + rows :] = zeros
        half[x, pad + rows :] = zeros

    def fill(i, carry):
        at = pl.multiple_of(i * pad, 8)
        for x in range(planes):
            field[x, pl.ds(pad + at, pad), :] = own[x, pl.ds(at, pad), :]
        return carry

    lax.fori_loop(0, blocks, fill, 0)

    def halve(i, carry):
        for x in range(planes):
            for o in range(group):
                tiles = [strided(field, x, i * pad + a * group + o) for a in range(4)]
                for a in range(3):
                    turned = pltpu.roll(jnp.where(left, tiles[a + 1], tiles[a]), 64, 1)
                    half[x, pl.ds(i * pad + a * group + o, 8, stride=step), :] = turned
        return carry

    lax.fori_loop(0, blocks + 1, halve, 0)

    def multiply(i):
        pieces = [
            jnp.concatenate(
                [strided(own, x, i * pad + a * group + o) for x in range(planes) for o in range(group)],
                axis=0,
            )
            for a in range(3)
        ]
        exact = jnp.concatenate(pieces, axis=1)
        high_part = exact.astype(jnp.bfloat16)
        low_part = (exact - high_part.astype(jnp.float32)).astype(jnp.bfloat16)
        return jnp.dot(
            jnp.concatenate([high_part, low_part, high_part], axis=1),
            line[...],
            preferred_element_type=jnp.float32,
        )

    def compute(i, part):
        for o in range(group):
            for a in range(3):
                at = i * pad + a * group + o
                column = [strided(own, x, at) for x in range(planes)]
                for x in range(planes):

                    def near(ref, tiles):
                        return strided(ref, x, pad + at + tiles * group)

                    row = (x * group + o) * 8
                    total = part[row : row + 8, 128 * a : 128 * a + 128]
                    total = total + scaled[x, pl.ds(i * 24 + a, 8, stride=3), :] * column[x]
                    pairs = (
                        near(half, 1) + near(half, -2),
                        near(field, 3) + near(field, -3),
                        near(half, 4) + near(half, -5),
                        near(field, 6) + near(field, -6),
                    )
                    for k in range(1, 5):
                        around = pairs[k - 1]
                        if x - k >= 0:
                            around = around + column[x - k]
                        if x + k < planes:
                            around = around + column[x + k]
                        total = total + weights[k] * around
                    if not first:
                        total = 2.0 * total - strided(before, x, at)
                    out[x, pl.ds(at, 8, stride=step), :] = total

    even[...] = multiply(0)

    def pair(i, carry):
        odd[...] = multiply(2 * i + 1)
        compute(2 * i, even)
        even[...] = multiply(jnp.minimum(2 * i + 2, blocks - 1))
        compute(2 * i + 1, odd)
        return carry

    lax.fori_loop(0, blocks // 2, pair, 0)


def inner(own, scaled, line, before, group):
    planes, rows, _ = own.shape
    first = before is None
    operands = (own, scaled, line) + (() if first else (before,))
    padded = (planes, rows + 48 * group, 128)
    return pl.pallas_call(
        functools.partial(inner_kernel, group=group, first=first),
        out_shape=jax.ShapeDtypeStruct(own.shape, jnp.float32),
        in_specs=[pl.BlockSpec(memory_space=pltpu.VMEM)] * len(operands),
        out_specs=pl.BlockSpec(memory_space=pltpu.VMEM),
        scratch_shapes=[
            pltpu.VMEM(padded, jnp.float32),
            pltpu.VMEM(padded, jnp.float32),
            pltpu.VMEM((planes * group * 8, 384), jnp.float32),
            pltpu.VMEM((planes * group * 8, 384), jnp.float32),
        ],
        name="inner_first" if first else "inner_next",
    )(*operands)


def edge_kernel(partial, low, top, out, *, factor):
    rows = partial.shape[1]

    def add(halo, nearby):
        def body(i, carry):
            at = pl.ds(pl.multiple_of(i * 8, 8), 8)
            beyond = [halo[x, at, :] for x in range(4)]
            for x in range(4):
                total = partial[x, at, :]
                for k in range(1, 5):
                    if nearby(x, k) is not None:
                        total = total + (factor * weights[k]) * beyond[nearby(x, k)]
                out[x, at, :] = total
            return carry

        lax.fori_loop(0, rows // 8, body, 0, unroll=4)

    @pl.when(pl.program_id(0) == 0)
    def _():
        add(low, lambda x, k: 4 + x - k if x < k else None)

    @pl.when(pl.program_id(0) == 1)
    def _():
        add(top, lambda x, k: x + k - 4 if x + k > 3 else None)


def edges(partial, low, top, factor):
    planes, rows, _ = partial.shape
    end = pl.BlockSpec((4, rows, 128), lambda i: (i * (planes // 4 - 1), 0, 0))
    halo = pl.BlockSpec((4, rows, 128), lambda i: (0, 0, 0))
    return pl.pallas_call(
        functools.partial(edge_kernel, factor=factor),
        grid=(2,),
        out_shape=jax.ShapeDtypeStruct(partial.shape, jnp.float32),
        in_specs=[end, halo, halo],
        out_specs=end,
        input_output_aliases={0: 0},
        name="edges",
    )(partial, low, top)


def rotate_kernel(picked, mixing, field, *outs):
    bands = len(outs)
    tiles = field.shape[1]

    def body(i, carry):
        at = pl.ds(pl.multiple_of(i * 8, 8), 8)

        def members(band):
            return [field[q * bands + band + 1 - 2 * (band % 2), at, :] for q in range(4)]

        shared = members(picked[0]) + members(picked[1])
        for k, out in enumerate(outs):
            own = members(picked[2] ^ k)
            for o in range(4):
                total = mixing[0, k, 0, o] * own[0]
                for q in range(1, 4):
                    total = total + mixing[0, k, q, o] * own[q]
                for t in range(2):
                    for q in range(4):
                        total = total + mixing[1 + t, k, q, o] * shared[4 * t + q]
                out[pl.ds(i * 32 + o, 8, stride=4), :] = total
        return carry

    lax.fori_loop(0, tiles // 8, body, 0)


def rotate(picked, mixing, field):
    count, tiles, _ = field.shape
    bands = count // 4
    return pl.pallas_call(
        rotate_kernel,
        out_shape=[jax.ShapeDtypeStruct((tiles * 4, 128), jnp.float32)] * bands,
        in_specs=[
            pl.BlockSpec(memory_space=pltpu.SMEM),
            pl.BlockSpec(memory_space=pltpu.SMEM),
            pl.BlockSpec(memory_space=pltpu.VMEM),
        ],
        out_specs=[pl.BlockSpec(memory_space=pltpu.VMEM)] * bands,
        name="rotate",
    )(picked, mixing, field)


AXES = ("domain", "band")


def split_kernel(orbit, rows, *outs):
    tiles = outs[0].shape[1]

    def body(i, carry):
        at = pl.ds(pl.multiple_of(i * 8, 8), 8)
        for k, out in enumerate(outs):
            out[0, at, :] = rows[0, pl.ds(i * 32 + orbit[k], 8, stride=4), :]
        return carry

    lax.fori_loop(0, tiles // 8, body, 0, unroll=4)


def split(orbit, rows):
    planes, count, _ = rows.shape
    small = pl.BlockSpec((1, count // 4, 128), lambda x: (x, 0, 0))
    return pl.pallas_call(
        split_kernel,
        grid=(planes,),
        out_shape=[jax.ShapeDtypeStruct((planes, count // 4, 128), jnp.float32)] * 4,
        in_specs=[pl.BlockSpec(memory_space=pltpu.SMEM), pl.BlockSpec((1, count, 128), lambda x: (x, 0, 0))],
        out_specs=[small] * 4,
        name="split",
    )(orbit, rows)


def merge_kernel(orbit, *refs):
    out = refs[-1]
    tiles = refs[0].shape[1]

    def body(i, carry):
        at = pl.ds(pl.multiple_of(i * 8, 8), 8)
        for k, part in enumerate(refs[:-1]):
            out[0, pl.ds(i * 32 + orbit[k], 8, stride=4), :] = part[0, at, :]
        return carry

    lax.fori_loop(0, tiles // 8, body, 0, unroll=4)


def merge(orbit, parts):
    planes, tiles, _ = parts[0].shape
    small = pl.BlockSpec((1, tiles, 128), lambda x: (x, 0, 0))
    return pl.pallas_call(
        merge_kernel,
        grid=(planes,),
        out_shape=jax.ShapeDtypeStruct((planes, tiles * 4, 128), jnp.float32),
        in_specs=[pl.BlockSpec(memory_space=pltpu.SMEM)] + [small] * 4,
        out_specs=pl.BlockSpec((1, tiles * 4, 128), lambda x: (x, 0, 0)),
        name="merge",
    )(orbit, *parts)


def place_kernel(slot, *refs):
    out, sems = refs[-2], refs[-1]
    planes = refs[0].shape[0]
    copies = [
        pltpu.make_async_copy(part, out.at[pl.ds(slot[k] * planes, planes)], sems.at[k])
        for k, part in enumerate(refs[:-2])
    ]
    for copy in copies:
        copy.start()
    for copy in copies:
        copy.wait()


def place(slot, parts):
    count, first = len(parts), parts[0].shape
    return pl.pallas_call(
        place_kernel,
        out_shape=jax.ShapeDtypeStruct((first[0] * count, *first[1:]), jnp.float32),
        in_specs=[pl.BlockSpec(memory_space=pltpu.SMEM)] + [pl.BlockSpec(memory_space=pl.ANY)] * count,
        out_specs=pl.BlockSpec(memory_space=pltpu.VMEM),
        scratch_shapes=[pltpu.SemaphoreType.DMA((count,))],
        name="place",
    )(slot, *parts)


def route(move):
    def at(x, y, z, c):
        return (z * 4 + y // 2 * 2 + c) * 8 + x * 2 + y % 2

    pairs = []
    for z in range(8):
        for y in range(4):
            for c in range(2):
                for x in range(4):
                    to_x, to_y, to_z, to_c = move(x, y, z, c)
                    pairs.append((at(x, y, z, c), at(to_x % 4, to_y % 4, to_z % 8, to_c % 2)))
    return pairs


def send(value, move):
    return lax.ppermute(value, AXES, route(move))


STEPS = ((1, 0), (1, 1), (-1, 0), (-1, 1))
ORBIT = np.array(
    [[[(y + dy) % 4 // 2 * 2 + (c + dc) % 2 for dy, dc in STEPS] for c in range(2)] for y in range(4)],
    np.int32,
)
SLOT = np.array(
    [[[(y - dy) % 4 // 2 * 2 + (c + dc) % 2 for dy, dc in STEPS] for c in range(2)] for y in range(4)],
    np.int32,
)


def whole_potential(slab, chip_x, high, core):
    planes, tiles, _ = slab.shape
    part = planes * tiles // 4
    mine = lax.dynamic_slice_in_dim(slab.reshape(4 * part, 128), chip_x * part, part)
    there = send(mine, lambda x, y, z, c: (x, y + (1 if y % 2 else -1), z, c))
    pieces = [there] + [send(there, lambda x, y, z, c, k=k: (x + k, y, z, c)) for k in range(1, 4)]
    stacked = jnp.stack(pieces)
    other = jnp.concatenate([lax.dynamic_index_in_dim(stacked, (chip_x - k) % 4, 0, False) for k in range(4)])
    other = other.reshape(slab.shape)
    both = jnp.where(high == 0, jnp.stack([slab, other]), jnp.stack([other, slab]))
    across = send(both, lambda x, y, z, c: (x, y, z, c + 1))
    cores = jnp.where(core == 0, jnp.stack([both, across], 1), jnp.stack([across, both], 1))
    return cores.reshape(4 * planes, tiles, 128)


def to_rows(block):
    width, planes, cells = block.shape
    tiles = block.reshape(width, planes, cells // 128, 128)
    return tiles.transpose(1, 2, 0, 3).reshape(planes, cells // 128 * width, 128)


def from_rows(rows, width):
    planes, count, _ = rows.shape
    tiles = rows.reshape(planes, count // width, width, 128).transpose(2, 0, 1, 3)
    return tiles.reshape(width, planes, count // width * 128)


def mixing_weights(coefficients, owners, width, bands):
    cut = coefficients.reshape(bands, width, bands, width)
    own = jnp.stack([cut[band, :, band, :] for band in range(bands)])
    parts = [own]
    for turn in range(2):
        source, offset = owners[turn] // width, owners[turn] % width
        rows = lax.dynamic_slice(coefficients, (source * width, 0), (width, bands * width))
        rows = jnp.roll(rows, offset, axis=0)
        parts.append(rows.reshape(width, bands, width).transpose(1, 0, 2))
    return jnp.stack(parts)


def body(orbitals, potential, coefficients, owners):
    width, planes, cells = orbitals.shape
    bands = lax.axis_size("band")
    tiles = cells // 128
    place_d, place_b = lax.axis_index("domain"), lax.axis_index("band")
    core, high, chip_x = place_d % 2, place_d // 2 % 2, place_b // 2
    chip_y = high * 2 + place_b % 2
    orbit = jnp.asarray(ORBIT)[chip_y, core]
    slot = jnp.asarray(SLOT)[chip_y, core]

    parts = split(orbit, to_rows(orbitals))
    parts = [
        send(part, lambda x, y, z, c, dy=dy, dc=dc: (x, y + dy, z, c + dc))
        for part, (dy, dc) in zip(parts, STEPS)
    ]
    scaled = (potential - 6.0) * 0.2 - 0.3 * lap_coeffs[0]
    scaled = whole_potential(scaled.reshape(planes, tiles, 128), chip_x, high, core)
    line = along_z()
    previous, current = None, place(slot, parts)
    for factor in (1.0, 2.0, 2.0):
        low = send(current[-4:], lambda x, y, z, c: (x, y, z + 1, c))
        top = send(current[:4], lambda x, y, z, c: (x, y, z - 1, c))
        partial = inner(current, scaled, line, previous, 1)
        previous, current = current, edges(partial, low, top, factor)

    layer = [[first + k for k in range(4 * bands)] for first in range(0, 32 * bands, 4 * bands)]
    gathered = lax.all_to_all(
        current.reshape(4 * bands, -1, 128), AXES, 0, 0, axis_index_groups=layer, tiled=True
    )
    mixing = mixing_weights(coefficients, owners, width, bands)
    mixing = jnp.concatenate(
        [lax.dynamic_slice_in_dim(mixing, place_b.astype(jnp.int32) ^ k, 1, 1) for k in range(bands)], axis=1
    )
    picked = jnp.concatenate([owners // width, place_b[None].astype(jnp.int32)])
    turned = rotate(picked, mixing, gathered)
    parts = [
        send(
            lax.dynamic_slice_in_dim(current, slot[k] * planes, planes),
            lambda x, y, z, c, dy=dy, dc=dc: (x, y - dy, z, c + dc),
        )
        for k, (dy, dc) in enumerate(STEPS)
    ]
    homes = list(turned)
    for k in (1, 3, 5, 7, 2, 4, 6):
        homes[k] = lax.ppermute(turned[k], "band", [(i, i ^ k) for i in range(bands)])
    filtered = from_rows(merge(orbit, parts), width)
    rotated = place(jnp.arange(bands, dtype=jnp.int32) ^ place_b.astype(jnp.int32), homes)
    rotated = from_rows(rotated.reshape(planes, tiles * width, 128), width)
    return (filtered, rotated)


def solution(mesh):
    in_specs = (P("band", "domain", None), P("domain", None), P(), P())
    out_specs = (P("band", "domain", None), P("band", "domain", None))
    return jax.shard_map(body, mesh=mesh, in_specs=in_specs, out_specs=out_specs, check_vma=False)
```
